256 devices in a mesh: island: 4 (over z_hi, core), tensor: 64 (over y, x, z_lo).
Axes of the slice: x: 4, y: 4, z: 8 (z_hi: 2, z_lo: 4; z = z_hi * 4 + z_lo), core: 2. Of those that a mesh axis runs over, the one named last changes fastest.
Arguments:
- activations: bfloat16 [4, 1024, 5120], P('island', 'tensor'), may hold values from -30 to 30, as said below
- cotangent: bfloat16 [4, 1024, 5120], P('island', 'tensor'), may hold values from -24 to 24
- gate_weight: bfloat16 [4, 6912, 5120], P('island', 'tensor'), may hold values from -6 to 6
- up_weight: bfloat16 [4, 6912, 5120], P('island', 'tensor'), may hold values from -6 to 6
- down_weight: bfloat16 [4, 6912, 5120], P('island', 'tensor'), may hold values from -6 to 6
- gate_control: bfloat16 [4, 6912, 5120], P('island', 'tensor'), may hold values from -4 to 4
- up_control: bfloat16 [4, 6912, 5120], P('island', 'tensor'), may hold values from -4 to 4
- down_control: bfloat16 [4, 6912, 5120], P('island', 'tensor'), may hold values from -4 to 4
Outputs:
- gate_new: bfloat16 [6912, 5120], P('tensor')
- up_new: bfloat16 [6912, 5120], P('tensor')
- down_new: bfloat16 [6912, 5120], P('tensor')
- gate_control_new: bfloat16 [4, 6912, 5120], P('island', 'tensor')
- up_control_new: bfloat16 [4, 6912, 5120], P('island', 'tensor')
- down_control_new: bfloat16 [4, 6912, 5120], P('island', 'tensor')
The draws below stay inside these ranges and needn't reach their ends.
Inputs may be any that keep to these rules, and one draw needn't show every extreme that they name: `activations`: real values; columns and tokens carry different scales.
All inputs are finite; a program needn't handle non-finite values.
Results may differ from the reference program's by a relative error of at most 0.0095.
Values may be sent and summed in bfloat16 or wider, within the bound.
No kernel may reach another device: no remote copies, remote signals or barrier semaphores. Data moves between devices by JAX's collectives and lax.ppermute only.
A program may use at most 128 MiB of HBM per device.

```python
import jax
import jax.numpy as jnp
from jax import lax

D = 5120
FF = 6912
ISLANDS = 4
TOKENS = 1024


def draw_activations(key, part):
    key_cols, key_rows, key_base = jax.random.split(key, 3)
    spread = jnp.log(10.0)
    column_scale = jnp.exp(jax.random.uniform(key_cols, (ISLANDS, 1, D), jnp.float32, 0.0, spread))
    row_scale = jnp.exp(jax.random.uniform(key_rows, (ISLANDS, TOKENS, 1), jnp.float32, 0.0, spread))
    base = jax.random.normal(key_base, (ISLANDS, TOKENS, D), jnp.float32)
    values = jnp.clip(0.3 * base * column_scale * row_scale, -30.0, 30.0)
    return values.astype(jnp.bfloat16)


def block_levels(rng, shape, shards, low, high):
    gain, own = 1.0, jax.random.fold_in(rng, 6)
    for position, shards_of in shards:
        steps = jnp.exp(jax.random.uniform(jax.random.fold_in(own, position), (shards_of,), jnp.float32, low / len(shards), high / len(shards)))
        gain = gain * jnp.repeat(steps, shape[position] // shards_of).reshape([-1 if axis == position else 1 for axis in range(len(shape))])
    return gain


def scatter_about(key, dims, scale, most, pieces=(), kind=jnp.bfloat16):
    entries = jax.random.normal(key, dims, jnp.float32) * scale
    if len(pieces) > 0:
        entries = block_levels(key, dims, pieces, -0.22, 0.18) * entries
    return jnp.clip(entries, min=-most, max=most).astype(kind)


def setup_inputs(seed: int = 0) -> dict:
    seeds = jax.random.split(jax.random.key(seed), 9)
    activations = draw_activations(jax.random.fold_in(seeds[8], 71), 0)
    cotangent = scatter_about(seeds[1], (ISLANDS, TOKENS, D), 4.0, 24.0, ((0, 4), (1, 64)))
    gate_weight = scatter_about(seeds[2], (ISLANDS, FF, D), 1.0, 6.0, ((0, 4), (1, 64)))
    up_weight = scatter_about(seeds[3], (ISLANDS, FF, D), 1.0, 6.0, ((0, 4), (1, 64)))
    down_weight = scatter_about(seeds[4], (ISLANDS, FF, D), 1.0, 6.0, ((0, 4), (1, 64)))
    gate_control = scatter_about(seeds[5], (ISLANDS, FF, D), 0.5, 4.0, ((0, 4), (1, 64)))
    up_control = scatter_about(seeds[6], (ISLANDS, FF, D), 0.5, 4.0, ((0, 4), (1, 64)))
    down_control = scatter_about(seeds[7], (ISLANDS, FF, D), 0.5, 4.0, ((0, 4), (1, 64)))
    return {"activations": activations, "cotangent": cotangent, "gate_weight": gate_weight, "up_weight": up_weight, "down_weight": down_weight, "gate_control": gate_control, "up_control": up_control, "down_control": down_control}


EPSILON = 1e-06
STEP_SIZE = 1.0
PROX_PROB = 0.5

def contract_first(left, right):
    return lax.dot_general(left, right, (((0,), (0,)), ((), ())), preferred_element_type=jnp.float32)

def contract_last(left, right):
    return lax.dot_general(left, right, (((1,), (1,)), ((), ())), preferred_element_type=jnp.float32)

def normalize(rows):
    wide = rows.astype(jnp.float32)
    mean_square = lax.optimization_barrier(jnp.mean(wide * wide, axis=-1, keepdims=True))
    return (wide * lax.rsqrt(mean_square + EPSILON)).astype(jnp.bfloat16)

def block_grads(normed, cot_rows, gate_w, up_w, down_w):
    d_scale = D ** (-0.5)
    f_scale = FF ** (-0.5)
    gate_proj = contract_last(normed, gate_w) * d_scale
    up_proj = contract_last(normed, up_w) * d_scale
    sigmoid_gate = jax.nn.sigmoid(gate_proj)
    activated = gate_proj * sigmoid_gate
    hidden = (activated * up_proj).astype(jnp.bfloat16)
    grad_down = contract_first(hidden, cot_rows) * f_scale
    grad_hidden = contract_last(cot_rows, down_w) * f_scale
    grad_gatepre = (grad_hidden * up_proj * sigmoid_gate * (1.0 + gate_proj * (1.0 - sigmoid_gate))).astype(jnp.bfloat16)
    grad_uppre = (grad_hidden * activated).astype(jnp.bfloat16)
    grad_gate = contract_first(grad_gatepre, normed) * d_scale
    grad_up = contract_first(grad_uppre, normed) * d_scale
    return (grad_gate, grad_up, grad_down)

def reference(activations, cotangent, gate_weight, up_weight, down_weight, gate_control, up_control, down_control):
    weights = (gate_weight, up_weight, down_weight)
    controls = (gate_control, up_control, down_control)
    locals_all = [[], [], []]
    terms_all = [[], [], []]
    for island in range(ISLANDS):
        normed = normalize(activations[island])
        grads = block_grads(normed, cotangent[island], gate_weight[island], up_weight[island], down_weight[island])
        for which in range(3):
            control = controls[which][island].astype(jnp.float32)
            local = weights[which][island].astype(jnp.float32) - STEP_SIZE * (grads[which] - control)
            locals_all[which].append(local)
            terms_all[which].append((local - STEP_SIZE / PROX_PROB * control).astype(jnp.bfloat16))
    averaged = []
    new_controls = []
    for which in range(3):
        total = lax.optimization_barrier(jnp.sum(jnp.stack([piece.astype(jnp.float32) for piece in terms_all[which]]), axis=0))
        mean_rounded = (total / ISLANDS).astype(jnp.bfloat16)
        averaged.append(mean_rounded)
        fresh = []
        for island in range(ISLANDS):
            control = controls[which][island].astype(jnp.float32)
            fresh.append((control + PROX_PROB / STEP_SIZE * (mean_rounded.astype(jnp.float32) - locals_all[which][island])).astype(jnp.bfloat16))
        new_controls.append(jnp.stack(fresh))
    return (averaged[0], averaged[1], averaged[2], new_controls[0], new_controls[1], new_controls[2])
```

```python
import jax
import jax.numpy as jnp
from jax import lax
from jax.sharding import PartitionSpec as P

D = 5120
FF = 6912
HALF = D // 2

EPSILON = 1e-06
STEP_SIZE = 1.0
PROX_PROB = 0.5

AXES = ("island", "tensor")


def device(y, x, z, core):
    return ((z // 4) * 2 + core) * 64 + y * 16 + x * 4 + z % 4


def shift(value, y=0, x=0, z_lo=0, z_hi=0, core=0):
    pairs = []
    for sy in range(4):
        for sx in range(4):
            for sz in range(8):
                for sc in range(2):
                    tz = (sz // 4 + z_hi) % 2 * 4 + (sz % 4 + z_lo) % 4
                    target = device((sy + y) % 4, (sx + x) % 4, tz, (sc + core) % 2)
                    pairs.append((device(sy, sx, sz, sc), target))
    return lax.ppermute(value, AXES, pairs)


def ring(block, axis):
    rows = block.shape[0] // 2
    from_low = shift(block, **{axis: 1})
    from_high = shift(block, **{axis: -1})
    far_top = shift(from_low[:rows], **{axis: 1})
    far_low = shift(from_high[rows:], **{axis: -1})
    return [[block], [from_low], [far_top, far_low], [from_high]]


def gather(rows, first, second):
    quads = [rows] + [shift(rows, z_lo=step) for step in (1, 2, 3)]
    block = jnp.concatenate(quads, axis=0)
    table = {}
    for i, pieces in enumerate(ring(block, first)):
        near = pieces[0] if len(pieces) == 1 else jnp.concatenate(pieces, axis=0)
        for j, far in enumerate(ring(near, second)):
            table[(i, j) if first == "y" else (j, i)] = far
    return [piece for key in sorted(table) for piece in table[key]]


def gather_both(rows):
    left = gather(rows[:, :HALF], "x", "y")
    right = gather(rows[:, HALF:], "y", "x")
    return jnp.concatenate(
        [jnp.concatenate(left, axis=0), jnp.concatenate(right, axis=0)], axis=1
    )


def contract_first(left, right):
    return lax.dot_general(
        left, right, (((0,), (0,)), ((), ())), preferred_element_type=jnp.float32
    )


def contract_last(left, right):
    return lax.dot_general(
        left, right, (((1,), (1,)), ((), ())), preferred_element_type=jnp.float32
    )


def normalize(rows):
    wide = rows.astype(jnp.float32)
    mean_square = jnp.mean(wide * wide, axis=-1, keepdims=True)
    return (wide * lax.rsqrt(mean_square + EPSILON)).astype(jnp.bfloat16)


def prox_parts(weight, control, grad):
    control_wide = control.astype(jnp.float32)
    local = weight.astype(jnp.float32) - STEP_SIZE * (grad - control_wide)
    return (local, (local - STEP_SIZE / PROX_PROB * control_wide).astype(jnp.bfloat16))


def island_mean(term, core):
    mine = lax.dynamic_slice_in_dim(term, core * HALF, HALF, axis=1)
    other = lax.dynamic_slice_in_dim(term, (1 - core) * HALF, HALF, axis=1)
    from_mate = shift(other, core=1)
    pair = (mine.astype(jnp.float32) + from_mate.astype(jnp.float32)).astype(jnp.bfloat16)
    pair = lax.optimization_barrier(pair)
    across = shift(pair, z_hi=1)
    mean = ((pair.astype(jnp.float32) + across.astype(jnp.float32)) / 4).astype(jnp.bfloat16)
    mate_mean = shift(mean, core=1)
    first = jnp.where(core == 0, mean, mate_mean)
    last = jnp.where(core == 0, mate_mean, mean)
    return jnp.concatenate([first, last], axis=1)


def fresh_control(control, mean_rounded, local):
    wide = control.astype(jnp.float32) + PROX_PROB / STEP_SIZE * (
        mean_rounded.astype(jnp.float32) - local
    )
    return wide.astype(jnp.bfloat16)[None]


def per_device(
    activations,
    cotangent,
    gate_weight,
    up_weight,
    down_weight,
    gate_control,
    up_control,
    down_control,
):
    d_scale = D ** (-0.5)
    f_scale = FF ** (-0.5)
    core = lax.axis_index("island") % 2
    normed = gather_both(normalize(activations[0]))
    cot = gather_both(cotangent[0])

    gate_proj = contract_last(normed, gate_weight[0]) * d_scale
    up_proj = contract_last(normed, up_weight[0]) * d_scale
    sigmoid_gate = jax.nn.sigmoid(gate_proj)
    activated = gate_proj * sigmoid_gate
    hidden = (activated * up_proj).astype(jnp.bfloat16)
    grad_down = contract_first(hidden, cot) * f_scale
    local_down, term_down = prox_parts(down_weight[0], down_control[0], grad_down)
    mean_down = island_mean(term_down, core)

    grad_hidden = contract_last(cot, down_weight[0]) * f_scale
    grad_gatepre = (
        grad_hidden * up_proj * sigmoid_gate * (1.0 + gate_proj * (1.0 - sigmoid_gate))
    ).astype(jnp.bfloat16)
    grad_uppre = (grad_hidden * activated).astype(jnp.bfloat16)
    grad_gate = contract_first(grad_gatepre, normed) * d_scale
    local_gate, term_gate = prox_parts(gate_weight[0], gate_control[0], grad_gate)
    mean_gate = island_mean(term_gate, core)
    grad_up = contract_first(grad_uppre, normed) * d_scale
    local_up, term_up = prox_parts(up_weight[0], up_control[0], grad_up)
    mean_up = island_mean(term_up, core)

    return (
        mean_gate,
        mean_up,
        mean_down,
        fresh_control(gate_control[0], mean_gate, local_gate),
        fresh_control(up_control[0], mean_up, local_up),
        fresh_control(down_control[0], mean_down, local_down),
    )


def solution(mesh):
    placed = (P("island", "tensor", None),) * 8
    return jax.shard_map(
        per_device,
        mesh=mesh,
        in_specs=placed,
        out_specs=(P("tensor", None),) * 3 + (P("island", "tensor", None),) * 3,
        check_vma=False,
    )
```

```python
import functools

import jax
import jax.numpy as jnp
from jax import lax
from jax.experimental import pallas as pl
from jax.experimental.pallas import tpu as pltpu
from jax.sharding import PartitionSpec as P


D = 5120
FF = 6912
HALF = D // 2
TOKENS = 1024
ROWS = FF // 64

EPSILON = 1e-06
STEP_SIZE = 1.0
PROX_PROB = 0.5

AXES = ("island", "tensor")
F32 = jnp.float32
BF16 = jnp.bfloat16


def device(y, x, z, core):
    return ((z // 4) * 2 + core) * 64 + y * 16 + x * 4 + z % 4


def shift(value, y=0, x=0, z_lo=0, z_hi=0, core=0):
    pairs = []
    for sy in range(4):
        for sx in range(4):
            for sz in range(8):
                for sc in range(2):
                    tz = (sz // 4 + z_hi) % 2 * 4 + (sz % 4 + z_lo) % 4
                    target = device((sy + y) % 4, (sx + x) % 4, tz, (sc + core) % 2)
                    pairs.append((device(sy, sx, sz, sc), target))
    return lax.ppermute(value, AXES, pairs)


def gather_line(rows):
    quads = [rows] + [shift(rows, z_lo=step) for step in (1, 2, 3)]
    return jnp.concatenate(quads, axis=0)


def ring(block, axis):
    low = shift(block, **{axis: 1})
    high = shift(block, **{axis: -1})
    far = shift(block, **{axis: 2})
    return [block, low, far, high]


def relay_near(block, axis):
    return shift(block, **{axis: 1}), shift(block, **{axis: -1})


def relay_far(block, near, axis):
    low, high = near
    rows = block.shape[0] // 2
    far_top = shift(low[:rows], **{axis: 1})
    far_low = shift(high[rows:], **{axis: -1})
    return [block, low, far_top, far_low, high]


def offsets(pieces):
    out, start = [], 0
    for piece in pieces:
        out.append((start, start + piece.shape[0], piece))
        start += piece.shape[0]
    return out


def swap(value):
    blocks = [value[64 * (4 * j + i) : 64 * (4 * j + i) + 64] for i in range(4) for j in range(4)]
    return jnp.concatenate(blocks, axis=0)


def dot_last(left, right):
    return lax.dot_general(left, right, (((1,), (1,)), ((), ())), preferred_element_type=F32)


def dot_inner(left, right):
    return lax.dot_general(left, right, (((1,), (0,)), ((), ())), preferred_element_type=F32)


def normalize(rows):
    wide = rows.astype(F32)
    mean_square = jnp.mean(wide * wide, axis=-1, keepdims=True)
    return (wide * lax.rsqrt(mean_square + EPSILON)).astype(BF16)


def whole(value):
    zeros = (0,) * value.ndim
    return pl.BlockSpec(value.shape, lambda g: zeros)


def columns(width, index):
    return pl.BlockSpec((1, ROWS, width), lambda g: (0, 0, index + g))


def shaped(rows, cols, dtype):
    return jax.ShapeDtypeStruct((rows, cols), dtype)


BLOCK = 640


def forward_kernel(*refs):
    lefts, rights = refs[:5], refs[5:10]
    weights, outs, sums = refs[10:14], refs[14:18], refs[18:22]
    hidden_l, hidden_r, gate_slope, up_slope = outs
    g = pl.program_id(0)

    def project(first):
        for pieces, pair in ((lefts, (0, 2)), (rights, (1, 3))):
            for start, stop, piece in offsets(pieces):
                value = piece[...]
                for k in pair:
                    now = dot_last(value, weights[k][0])
                    sums[k][start:stop] = now if first else sums[k][start:stop] + now

    pl.when(g == 0)(lambda: project(True))
    pl.when(g > 0)(lambda: project(False))

    @pl.when(g == HALF // BLOCK - 1)
    def _():
        scale = D ** (-0.5)
        gate = (sums[0][...] + swap(sums[1][...])) * scale
        up = (sums[2][...] + swap(sums[3][...])) * scale
        sigmoid = jax.nn.sigmoid(gate)
        activated = gate * sigmoid
        hidden = activated * up
        hidden_l[...] = hidden.T.astype(BF16)
        hidden_r[...] = swap(hidden).T.astype(BF16)
        gate_slope[...] = up * sigmoid * (1.0 + gate * (1.0 - sigmoid))
        up_slope[...] = activated


def strips(value):
    return pl.BlockSpec((value.shape[0], BLOCK), lambda g: (0, g))


def forward_call(lefts, rights, gate_w, up_w):
    out = (shaped(ROWS, TOKENS, BF16),) * 2 + (shaped(TOKENS, ROWS, F32),) * 2
    return pl.pallas_call(
        forward_kernel,
        out_shape=out,
        grid=(HALF // BLOCK,),
        in_specs=[strips(v) for v in (*lefts, *rights)]
        + [columns(BLOCK, 0), columns(BLOCK, HALF // BLOCK)] * 2,
        out_specs=tuple(whole(v) for v in out),
        scratch_shapes=[pltpu.VMEM((TOKENS, ROWS), F32)] * 4,
    )(*lefts, *rights, gate_w, gate_w, up_w, up_w)


def backward_kernel(*refs):
    parts_l, parts_r = refs[0:2], refs[2:4]
    gate_slope, up_slope, gate_pl, gate_pr, up_pl, up_pr = refs[4:]
    left = parts_l[0][...] + parts_l[1][...]
    right = parts_r[0][...] + parts_r[1][...]
    grad = (left + swap(right)) * FF ** (-0.5)
    gate = grad * gate_slope[...]
    up = grad * up_slope[...]
    gate_pl[...] = gate.T.astype(BF16)
    gate_pr[...] = swap(gate).T.astype(BF16)
    up_pl[...] = up.T.astype(BF16)
    up_pr[...] = swap(up).T.astype(BF16)


def backward_call(*args):
    return pl.pallas_call(backward_kernel, out_shape=(shaped(ROWS, TOKENS, BF16),) * 4)(*args)


def grads_kernel(scale, with_parts, core, pre_l, pre_r, *refs):
    lefts, rights = refs[:5], refs[5:10]
    w_l, w_r, c_l, c_r, mine, other, local_l, local_r = refs[10:18]
    parts = refs[18:]
    terms = []
    for pre, pieces, w, c, local in (
        (pre_l, lefts, w_l, c_l, local_l),
        (pre_r, rights, w_r, c_r, local_r),
    ):
        total = None
        for start, stop, piece in offsets(pieces):
            now = dot_inner(pre[:, start:stop], piece[...])
            total = now if total is None else total + now
        control = c[0].astype(F32)
        new = w[0].astype(F32) - STEP_SIZE * (total * scale - control)
        local[...] = new
        terms.append((new - STEP_SIZE / PROX_PROB * control).astype(BF16))
    first = core[0] == 0
    mine[...] = jnp.where(first, terms[0], terms[1])
    other[...] = jnp.where(first, terms[1], terms[0])
    if with_parts:
        g = pl.program_id(0)

        def project(begin):
            for pieces, w, part in ((lefts, w_l, parts[0]), (rights, w_r, parts[1])):
                for start, stop, piece in offsets(pieces):
                    now = dot_last(piece[...], w[0])
                    part[start:stop] = now if begin else part[start:stop] + now

        pl.when(g == 0)(lambda: project(True))
        pl.when(g > 0)(lambda: project(False))


def grads_call(core, pre_l, pre_r, lefts, rights, weight, control, block, scale, with_parts):
    width = lefts[0].shape[1]
    at = block * width // BLOCK
    args = (pre_l, pre_r, *lefts, *rights)
    specs = [whole(pre_l), whole(pre_r)] + [strips(v) for v in (*lefts, *rights)]
    specs += [columns(BLOCK, at), columns(BLOCK, HALF // BLOCK + at)] * 2
    out = [shaped(ROWS, width, BF16)] * 2 + [shaped(ROWS, width, F32)] * 2
    out_specs = [strips(v) for v in out]
    if with_parts:
        sums = [shaped(TOKENS, ROWS, F32)] * 2
        out, out_specs = out + sums, out_specs + [whole(v) for v in sums]
    return pl.pallas_call(
        functools.partial(grads_kernel, scale, with_parts),
        out_shape=out,
        grid=(width // BLOCK,),
        in_specs=[pl.BlockSpec(memory_space=pltpu.SMEM)] + specs,
        out_specs=out_specs,
    )(core, *args, weight, weight, control, control)


def island_mean(mine, other):
    from_mate = shift(other, core=1)
    pair = (mine.astype(F32) + from_mate.astype(F32)).astype(BF16)
    pair = lax.optimization_barrier(pair)
    across = shift(pair, z_hi=1)
    mean = ((pair.astype(F32) + across.astype(F32)) / 4).astype(BF16)
    return mean, shift(mean, core=1)


def finish_kernel(count, core, *refs):
    means, mates, locals_l, locals_r = (refs[k * count : (k + 1) * count] for k in range(4))
    control, mean_out, fresh_out = refs[4 * count :]
    first = core[0] == 0
    width = means[0].shape[1]
    for k in range(count):
        mean, mate = means[k][...], mates[k][...]
        sides = (
            (k * width, jnp.where(first, mean, mate), locals_l[k]),
            (HALF + k * width, jnp.where(first, mate, mean), locals_r[k]),
        )
        for start, value, local in sides:
            at = slice(start, start + width)
            mean_out[:, at] = value
            old = control[0, :, at].astype(F32)
            step = PROX_PROB / STEP_SIZE * (value.astype(F32) - local[...])
            fresh_out[0, :, at] = (old + step).astype(BF16)


def finish_call(core, blocks, control):
    args = [block[k] for k in range(4) for block in blocks] + [control]
    out = (shaped(ROWS, D, BF16), jax.ShapeDtypeStruct((1, ROWS, D), BF16))
    return pl.pallas_call(
        functools.partial(finish_kernel, len(blocks)),
        out_shape=out,
        grid=(1,),
        in_specs=[pl.BlockSpec(memory_space=pltpu.SMEM)] + [whole(v) for v in args],
        out_specs=tuple(whole(v) for v in out),
    )(core, *args)


def per_device(
    activations,
    cotangent,
    gate_weight,
    up_weight,
    down_weight,
    gate_control,
    up_control,
    down_control,
):
    d_scale = D ** (-0.5)
    f_scale = FF ** (-0.5)
    core = jnp.full((1,), lax.axis_index("island") % 2, jnp.int32)
    line = gather_line(normalize(activations[0]))
    four_left = jnp.concatenate(ring(line[:, :HALF], "x"), axis=0)
    four_right = jnp.concatenate(ring(line[:, HALF:], "y"), axis=0)
    near_left = relay_near(four_left, "y")
    near_right = relay_near(four_right, "x")
    lefts = relay_far(four_left, near_left, "y")
    rights = relay_far(four_right, near_right, "x")

    cot_line = gather_line(cotangent[0])
    cot_ring_left = ring(cot_line[:, :HALF], "x")
    cot_ring_right = ring(cot_line[:, HALF:], "y")
    cot = []
    size = HALF // 2
    for i in range(2):
        at = slice(i * size, i * size + size)
        left = jnp.concatenate([v[:, at] for v in cot_ring_left], axis=0)
        right = jnp.concatenate([v[:, at] for v in cot_ring_right], axis=0)
        near_l = relay_near(left, "y")
        near_r = relay_near(right, "x")
        cot.append((relay_far(left, near_l, "y"), relay_far(right, near_r, "x")))

    hidden_l, hidden_r, gate_slope, up_slope = forward_call(lefts, rights, gate_weight, up_weight)
    down_blocks, parts = [], []
    for i in range(2):
        mine, other, local_l, local_r, *part = grads_call(
            core, hidden_l, hidden_r, *cot[i], down_weight, down_control, i, f_scale, True
        )
        parts.append(part)
        down_blocks.append((*island_mean(mine, other), local_l, local_r))
    gate_pl, gate_pr, up_pl, up_pr = backward_call(
        parts[0][0], parts[1][0], parts[0][1], parts[1][1], gate_slope, up_slope
    )
    outs = {}
    for name, pre_l, pre_r, weight, control in (
        ("gate", gate_pl, gate_pr, gate_weight, gate_control),
        ("up", up_pl, up_pr, up_weight, up_control),
    ):
        mine, other, local_l, local_r = grads_call(
            core, pre_l, pre_r, lefts, rights, weight, control, 0, d_scale, False
        )
        blocks = [(*island_mean(mine, other), local_l, local_r)]
        outs[name] = finish_call(core, blocks, control)
    mean_down, fresh_down = finish_call(core, down_blocks, down_control)
    return (
        outs["gate"][0],
        outs["up"][0],
        mean_down,
        outs["gate"][1],
        outs["up"][1],
        fresh_down,
    )


def solution(mesh):
    placed = (P("island", "tensor", None),) * 8
    return jax.shard_map(
        per_device,
        mesh=mesh,
        in_specs=placed,
        out_specs=(P("tensor", None),) * 3 + (P("island", "tensor", None),) * 3,
        check_vma=False,
    )
```

```python
import functools

import jax
import jax.numpy as jnp
from jax import lax
from jax.experimental import pallas as pl
from jax.experimental.pallas import tpu as pltpu
from jax.sharding import PartitionSpec as P


D = 5120
FF = 6912
HALF = D // 2
TOKENS = 1024
ROWS = FF // 64

EPSILON = 1e-06
STEP_SIZE = 1.0
PROX_PROB = 0.5

AXES = ("island", "tensor")
F32 = jnp.float32
BF16 = jnp.bfloat16


def device(y, x, z, core):
    return ((z // 4) * 2 + core) * 64 + y * 16 + x * 4 + z % 4


def shift(value, y=0, x=0, z_lo=0, z_hi=0, core=0):
    pairs = []
    for sy in range(4):
        for sx in range(4):
            for sz in range(8):
                for sc in range(2):
                    tz = (sz // 4 + z_hi) % 2 * 4 + (sz % 4 + z_lo) % 4
                    target = device((sy + y) % 4, (sx + x) % 4, tz, (sc + core) % 2)
                    pairs.append((device(sy, sx, sz, sc), target))
    return lax.ppermute(value, AXES, pairs)


def gather_line(rows):
    return [rows] + [shift(rows, z_lo=step) for step in (1, 2, 3)]


def ring(block, axis):
    low = shift(block, **{axis: 1})
    high = shift(block, **{axis: -1})
    far = shift(block, **{axis: 2})
    return [block, low, far, high]


def join_kernel(*refs):
    quads, left, right = refs[:4], refs[4], refs[5]
    for k, quad in enumerate(quads):
        at = slice(64 * k, 64 * k + 64)
        left[at] = quad[:, :WIDTH]
        right[at] = quad[:, WIDTH:]


def join_call(quads):
    return pl.pallas_call(join_kernel, out_shape=(shaped(256, WIDTH, BF16),) * 2)(*quads)


def relay_near(block, axis):
    return shift(block, **{axis: 1}), shift(block, **{axis: -1})


def relay_far(block, near, axis):
    low, high = near
    rows = block.shape[0] // 2
    far_top = shift(low[:rows], **{axis: 1})
    far_low = shift(high[rows:], **{axis: -1})
    return [block, low, far_top, far_low, high]


def relay_over(value, axis, step):
    return shift(value, **{axis: step})


def offsets(pieces):
    out, start = [], 0
    for piece in pieces:
        out.append((start, start + piece.shape[0], piece))
        start += piece.shape[0]
    return out


def reorder(value, held, wanted):
    places = [dict(zip(wanted, (i, j, k))) for i in range(4) for j in range(4) for k in range(4)]
    starts = [16 * (16 * p[held[0]] + 4 * p[held[1]] + p[held[2]]) for p in places]
    return jnp.concatenate([value[s : s + 16] for s in starts], axis=0)


def dot_last(left, right):
    return lax.dot_general(left, right, (((1,), (1,)), ((), ())), preferred_element_type=F32)


def dot_inner(left, right):
    return lax.dot_general(left, right, (((1,), (0,)), ((), ())), preferred_element_type=F32)


def normalize(rows):
    wide = rows.astype(F32)
    mean_square = jnp.mean(wide * wide, axis=-1, keepdims=True)
    return (wide * lax.rsqrt(mean_square + EPSILON)).astype(BF16)


def whole(value):
    zeros = (0,) * value.ndim
    return pl.BlockSpec(value.shape, lambda g: zeros)


def columns(width, index):
    return pl.BlockSpec((1, ROWS, width), lambda g: (0, 0, index + g))


def shaped(rows, cols, dtype):
    return jax.ShapeDtypeStruct((rows, cols), dtype)


BLOCK = 640


def forward_kernel(*refs):
    lefts, rights = refs[:5], refs[5:10]
    weights, outs, sums = refs[10:14], refs[14:18], refs[18:20]
    hidden_l, hidden_r, gate_slope, up_slope = outs
    g = pl.program_id(0)
    gap = jnp.zeros((128 - ROWS, BLOCK), BF16)

    def project(first):
        for k, pieces in enumerate((lefts, rights)):
            joint = jnp.concatenate([weights[k][0], gap, weights[2 + k][0], gap], axis=0)
            for start, stop, piece in offsets(pieces):
                now = dot_last(piece[...], joint)
                sums[k][start:stop] = now if first else sums[k][start:stop] + now

    pl.when(g == 0)(lambda: project(True))
    pl.when(g > 0)(lambda: project(False))

    @pl.when(g == HALF // BLOCK - 1)
    def _():
        scale = D ** (-0.5)
        gate = (sums[0][:, :ROWS] + reorder(sums[1][:, :ROWS], "xyz", "yxz")) * scale
        up = (sums[0][:, 128 : 128 + ROWS] + reorder(sums[1][:, 128 : 128 + ROWS], "xyz", "yxz")) * scale
        sigmoid = jax.nn.sigmoid(gate)
        activated = gate * sigmoid
        hidden = activated * up
        hidden_l[...] = reorder(hidden, "yxz", "yzx").T.astype(BF16)
        hidden_r[...] = reorder(hidden, "yxz", "xzy").T.astype(BF16)
        gate_slope[...] = up * sigmoid * (1.0 + gate * (1.0 - sigmoid))
        up_slope[...] = activated


def strips(value):
    return pl.BlockSpec((value.shape[0], BLOCK), lambda g: (0, g))


def forward_call(lefts, rights, gate_w, up_w):
    out = (shaped(ROWS, TOKENS, BF16),) * 2 + (shaped(TOKENS, ROWS, F32),) * 2
    return pl.pallas_call(
        forward_kernel,
        out_shape=out,
        grid=(HALF // BLOCK,),
        in_specs=[strips(v) for v in (*lefts, *rights)]
        + [columns(BLOCK, 0), columns(BLOCK, HALF // BLOCK)] * 2,
        out_specs=tuple(whole(v) for v in out),
        scratch_shapes=[pltpu.VMEM((TOKENS, 256), F32)] * 2,
    )(*lefts, *rights, gate_w, gate_w, up_w, up_w)


PAD = 112


def backward_kernel(*refs):
    parts_l, parts_r = refs[0:2], refs[2:4]
    gate_slope, up_slope, pre_l, pre_r = refs[4:]
    left = parts_l[0][...] + parts_l[1][...]
    right = parts_r[0][...] + parts_r[1][...]
    grad = reorder(left, "yzx", "yxz") + reorder(right, "xzy", "yxz")
    grad = grad * FF ** (-0.5)
    gap = jnp.zeros((PAD - ROWS, TOKENS), BF16)
    gate = grad * gate_slope[...]
    up = grad * up_slope[...]
    for out, order in ((pre_l, "yxz"), (pre_r, "xyz")):
        gate_rows = reorder(gate, "yxz", order).T.astype(BF16)
        up_rows = reorder(up, "yxz", order).T.astype(BF16)
        out[...] = jnp.concatenate([gate_rows, gap, up_rows, gap], axis=0)


def backward_call(*args):
    out = (shaped(2 * PAD, TOKENS, BF16),) * 2
    return pl.pallas_call(backward_kernel, out_shape=out)(*args)


def grads_kernel(scale, count, pieces, with_parts, core, pre_l, pre_r, *refs):
    lefts, rights, refs = refs[:pieces], refs[pieces : 2 * pieces], refs[2 * pieces :]
    weights, controls, refs = refs[: 2 * count], refs[2 * count : 4 * count], refs[4 * count :]
    mine, other, local, *parts = refs
    terms = []
    for side, pre, blocks in ((0, pre_l, lefts), (1, pre_r, rights)):
        total = None
        for start, stop, piece in offsets(blocks):
            now = dot_inner(pre[:, start:stop], piece[...])
            total = now if total is None else total + now
        for k in range(count):
            control = controls[2 * k + side][0].astype(F32)
            grad = total[PAD * k : PAD * k + ROWS] * scale
            new = weights[2 * k + side][0].astype(F32) - STEP_SIZE * (grad - control)
            local[side, k] = new
            terms.append((new - STEP_SIZE / PROX_PROB * control).astype(BF16))
    first = core[0] == 0
    gap = jnp.zeros((PAD - ROWS, BLOCK), BF16)
    for k in range(count):
        at = slice(PAD * k, PAD * k + PAD)
        left, right = (jnp.concatenate([terms[n], gap], axis=0) for n in (k, count + k))
        mine[at] = jnp.where(first, left, right)
        other[at] = jnp.where(first, right, left)
    if with_parts:
        g = pl.program_id(0)

        def project(begin):
            for blocks, w, part in ((lefts, weights[0], parts[0]), (rights, weights[1], parts[1])):
                for start, stop, piece in offsets(blocks):
                    now = dot_last(piece[...], w[0])
                    part[start:stop] = now if begin else part[start:stop] + now

        pl.when(g == 0)(lambda: project(True))
        pl.when(g > 0)(lambda: project(False))


WIDTH = HALF // 2


def grads_call(core, pre_l, pre_r, lefts, rights, weights, controls, block, scale, with_parts):
    count = len(weights)
    at = block * WIDTH // BLOCK
    own = at if lefts[0].shape[1] == HALF else 0
    args = (*lefts, *rights)
    specs = [whole(pre_l), whole(pre_r)]
    specs += [pl.BlockSpec((v.shape[0], BLOCK), lambda g: (0, own + g)) for v in args]
    specs += [columns(BLOCK, at), columns(BLOCK, HALF // BLOCK + at)] * (2 * count)
    out = [shaped(count * PAD, WIDTH, BF16)] * 2
    out_specs = [strips(v) for v in out]
    out += [jax.ShapeDtypeStruct((2, count, ROWS, WIDTH), F32)]
    out_specs += [pl.BlockSpec((2, count, ROWS, BLOCK), lambda g: (0, 0, 0, g))]
    if with_parts:
        sums = [shaped(TOKENS, ROWS, F32)] * 2
        out, out_specs = out + sums, out_specs + [whole(v) for v in sums]
    doubled = [v for v in (*weights, *controls) for _ in range(2)]
    return pl.pallas_call(
        functools.partial(grads_kernel, scale, count, len(lefts), with_parts),
        out_shape=out,
        grid=(WIDTH // BLOCK,),
        in_specs=[pl.BlockSpec(memory_space=pltpu.SMEM)] + specs,
        out_specs=out_specs,
    )(core, pre_l, pre_r, *args, *doubled)


def island_mean(mine, other):
    from_mate = shift(other, core=1)
    pair = (mine.astype(F32) + from_mate.astype(F32)).astype(BF16)
    pair = lax.optimization_barrier(pair)
    across = shift(pair, z_hi=1)
    mean = ((pair.astype(F32) + across.astype(F32)) / 4).astype(BF16)
    return mean, shift(mean, core=1)


def finish_kernel(count, core, mean, mate, local, *refs):
    controls, outs = refs[:count], refs[-2 * count :]
    straight = (core[0] == 0) == (pl.program_id(0) == 0)
    for k in range(count):
        rows = slice(PAD * k, PAD * k + ROWS)
        value = jnp.where(straight, mean[rows], mate[rows])
        outs[2 * k][...] = value
        step = PROX_PROB / STEP_SIZE * (value.astype(F32) - local[0, k])
        outs[2 * k + 1][0] = (controls[k][0].astype(F32) + step).astype(BF16)


def finish_call(core, block, mean, mate, local, controls, before):
    count = len(controls)
    out = [shaped(ROWS, D, BF16), jax.ShapeDtypeStruct((1, ROWS, D), BF16)] * count
    spot = pl.BlockSpec((ROWS, WIDTH), lambda g: (0, 2 * g + block))
    spot3 = pl.BlockSpec((1, ROWS, WIDTH), lambda g: (0, 0, 2 * g + block))
    specs = [pl.BlockSpec(memory_space=pltpu.SMEM), whole(mean), whole(mate)]
    specs += [pl.BlockSpec((1, count, ROWS, WIDTH), lambda g: (g, 0, 0, 0))]
    specs += [spot3] * count + [pl.BlockSpec(memory_space=pl.ANY)] * len(before)
    return pl.pallas_call(
        functools.partial(finish_kernel, count),
        out_shape=out,
        grid=(2,),
        in_specs=specs,
        out_specs=[spot, spot3] * count,
        input_output_aliases={4 + count + i: i for i in range(len(before))},
    )(core, mean, mate, local, *controls, *before)


def per_device(
    activations,
    cotangent,
    gate_weight,
    up_weight,
    down_weight,
    gate_control,
    up_control,
    down_control,
):
    d_scale = D ** (-0.5)
    f_scale = FF ** (-0.5)
    core = jnp.full((1,), lax.axis_index("island") % 2, jnp.int32)
    line = jnp.concatenate(gather_line(normalize(activations[0])), axis=0)
    four_left = jnp.concatenate(ring(line[:, :HALF], "x"), axis=0)
    four_right = jnp.concatenate(ring(line[:, HALF:], "y"), axis=0)
    near_left = relay_near(four_left, "y")
    near_right = relay_near(four_right, "x")
    lefts = relay_far(four_left, near_left, "y")
    rights = relay_far(four_right, near_right, "x")

    rows = cotangent[0]
    ring_left, ring_right = ring(rows[:, :HALF], "x"), ring(rows[:, HALF:], "y")
    cot = []
    for i in range(2):
        at = slice(i * WIDTH, i * WIDTH + WIDTH)
        four = [
            jnp.concatenate([v[:, at] for v in quads], axis=0)
            for quads in (ring_left, ring_right)
        ]
        four = jnp.concatenate(four, axis=1)
        quads = gather_line(four)
        joined = join_call(quads)
        sides = []
        for block, axis in zip(joined, ("y", "x")):
            low = relay_over(block, axis, 1)
            high = relay_over(block, axis, -1)
            far = relay_over(low, axis, 1) if i == 0 else relay_over(high, axis, -1)
            sides.append([block, low, far, high])
        cot.append(sides)

    hidden_l, hidden_r, gate_slope, up_slope = forward_call(lefts, rights, gate_weight, up_weight)
    parts, down = [], []
    for i in range(2):
        mine, other, local, *part = grads_call(
            core, hidden_l, hidden_r, *cot[i], [down_weight], [down_control], i, f_scale, True
        )
        parts.append(part)
        mean, mate = island_mean(mine, other)
        down = finish_call(core, i, mean, mate, local, [down_control], down)
    pre_l, pre_r = backward_call(
        parts[0][0], parts[1][0], parts[0][1], parts[1][1], gate_slope, up_slope
    )
    both = []
    controls = [gate_control, up_control]
    for i in range(2):
        mine, other, local = grads_call(
            core, pre_l, pre_r, lefts, rights, [gate_weight, up_weight], controls, i, d_scale, False
        )
        mean, mate = island_mean(mine, other)
        both = finish_call(core, i, mean, mate, local, controls, both)
    return (both[0], both[2], down[0], both[1], both[3], down[1])


def solution(mesh):
    placed = (P("island", "tensor", None),) * 8
    return jax.shard_map(
        per_device,
        mesh=mesh,
        in_specs=placed,
        out_specs=(P("tensor", None),) * 3 + (P("island", "tensor", None),) * 3,
        check_vma=False,
    )
```

```python
import functools

import jax
import jax.numpy as jnp
from jax import lax
from jax.experimental import pallas as pl
from jax.experimental.pallas import tpu as pltpu
from jax.sharding import PartitionSpec as P


D = 5120
FF = 6912
HALF = D // 2
TOKENS = 1024
ROWS = FF // 64

EPSILON = 1e-06
STEP_SIZE = 1.0
PROX_PROB = 0.5

AXES = ("island", "tensor")
F32 = jnp.float32
BF16 = jnp.bfloat16


def device(y, x, z, core):
    return ((z // 4) * 2 + core) * 64 + y * 16 + x * 4 + z % 4


def shift(value, y=0, x=0, z_lo=0, z_hi=0, core=0):
    pairs = []
    for sy in range(4):
        for sx in range(4):
            for sz in range(8):
                for sc in range(2):
                    tz = (sz // 4 + z_hi) % 2 * 4 + (sz % 4 + z_lo) % 4
                    target = device((sy + y) % 4, (sx + x) % 4, tz, (sc + core) % 2)
                    pairs.append((device(sy, sx, sz, sc), target))
    return lax.ppermute(value, AXES, pairs)


def gather_line(rows):
    return [rows] + [shift(rows, z_lo=step) for step in (1, 2, 3)]


def ring(block, axis):
    low = shift(block, **{axis: 1})
    high = shift(block, **{axis: -1})
    far = shift(block, **{axis: 2})
    return [block, low, far, high]


def join_kernel(*refs):
    quads, left, right = refs[:4], refs[4], refs[5]
    for k, quad in enumerate(quads):
        at = slice(64 * k, 64 * k + 64)
        left[at] = quad[:, :WIDTH]
        right[at] = quad[:, WIDTH:]


def join_call(quads):
    return pl.pallas_call(join_kernel, out_shape=(shaped(256, WIDTH, BF16),) * 2)(*quads)


def relay_near(block, axis):
    return shift(block, **{axis: 1}), shift(block, **{axis: -1})


def relay_far(block, near, axis):
    low, high = near
    rows = block.shape[0] // 2
    far_top = shift(low[:rows], **{axis: 1})
    far_low = shift(high[rows:], **{axis: -1})
    return [block, low, far_top, far_low, high]


def relay_over(value, axis, step):
    return shift(value, **{axis: step})


def offsets(pieces):
    out, start = [], 0
    for piece in pieces:
        out.append((start, start + piece.shape[0], piece))
        start += piece.shape[0]
    return out


def reorder(value, held, wanted):
    places = [dict(zip(wanted, (i, j, k))) for i in range(4) for j in range(4) for k in range(4)]
    starts = [16 * (16 * p[held[0]] + 4 * p[held[1]] + p[held[2]]) for p in places]
    return jnp.concatenate([value[s : s + 16] for s in starts], axis=0)


def dot_last(left, right):
    return lax.dot_general(left, right, (((1,), (1,)), ((), ())), preferred_element_type=F32)


def dot_inner(left, right):
    return lax.dot_general(left, right, (((1,), (0,)), ((), ())), preferred_element_type=F32)


def normalize(rows):
    wide = rows.astype(F32)
    mean_square = jnp.mean(wide * wide, axis=-1, keepdims=True)
    return (wide * lax.rsqrt(mean_square + EPSILON)).astype(BF16)


def whole(value):
    zeros = (0,) * value.ndim
    return pl.BlockSpec(value.shape, lambda g: zeros)


def columns(width, index):
    return pl.BlockSpec((1, ROWS, width), lambda g: (0, 0, index + g))


def shaped(rows, cols, dtype):
    return jax.ShapeDtypeStruct((rows, cols), dtype)


BLOCK = 640


def forward_kernel(*refs):
    lefts, rights = refs[:5], refs[5:10]
    weights, outs, sums = refs[10:14], refs[14:18], refs[18:20]
    hidden_l, hidden_r, gate_slope, up_slope = outs
    g = pl.program_id(0)
    gap = jnp.zeros((128 - ROWS, BLOCK), BF16)

    def project(first):
        for k, pieces in enumerate((lefts, rights)):
            joint = jnp.concatenate([weights[k][0], gap, weights[2 + k][0], gap], axis=0)
            for start, stop, piece in offsets(pieces):
                now = dot_last(piece[...], joint)
                sums[k][start:stop] = now if first else sums[k][start:stop] + now

    pl.when(g == 0)(lambda: project(True))
    pl.when(g > 0)(lambda: project(False))

    @pl.when(g == HALF // BLOCK - 1)
    def _():
        scale = D ** (-0.5)
        gate = (sums[0][:, :ROWS] + reorder(sums[1][:, :ROWS], "xyz", "yxz")) * scale
        up = (sums[0][:, 128 : 128 + ROWS] + reorder(sums[1][:, 128 : 128 + ROWS], "xyz", "yxz")) * scale
        sigmoid = jax.nn.sigmoid(gate)
        activated = gate * sigmoid
        hidden = activated * up
        hidden_l[...] = reorder(hidden, "yxz", "yzx").T.astype(BF16)
        hidden_r[...] = reorder(hidden, "yxz", "xzy").T.astype(BF16)
        gate_slope[...] = up * sigmoid * (1.0 + gate * (1.0 - sigmoid))
        up_slope[...] = activated


def strips(value):
    return pl.BlockSpec((value.shape[0], BLOCK), lambda g: (0, g))


def forward_call(lefts, rights, gate_w, up_w):
    out = (shaped(ROWS, TOKENS, BF16),) * 2 + (shaped(TOKENS, ROWS, F32),) * 2
    return pl.pallas_call(
        forward_kernel,
        out_shape=out,
        grid=(HALF // BLOCK,),
        in_specs=[strips(v) for v in (*lefts, *rights)]
        + [columns(BLOCK, 0), columns(BLOCK, HALF // BLOCK)] * 2,
        out_specs=tuple(whole(v) for v in out),
        scratch_shapes=[pltpu.VMEM((TOKENS, 256), F32)] * 2,
    )(*lefts, *rights, gate_w, gate_w, up_w, up_w)


PAD = 112


def backward_kernel(*refs):
    parts_l, parts_r = refs[0:2], refs[2:4]
    gate_slope, up_slope, pre_l, pre_r = refs[4:]
    left = parts_l[0][...] + parts_l[1][...]
    right = parts_r[0][...] + parts_r[1][...]
    grad = reorder(left, "yzx", "yxz") + reorder(right, "xzy", "yxz")
    grad = grad * FF ** (-0.5)
    gap = jnp.zeros((PAD - ROWS, TOKENS), BF16)
    gate = grad * gate_slope[...]
    up = grad * up_slope[...]
    for out, order in ((pre_l, "yxz"), (pre_r, "xyz")):
        gate_rows = reorder(gate, "yxz", order).T.astype(BF16)
        up_rows = reorder(up, "yxz", order).T.astype(BF16)
        out[...] = jnp.concatenate([gate_rows, gap, up_rows, gap], axis=0)


def backward_call(*args):
    out = (shaped(2 * PAD, TOKENS, BF16),) * 2
    return pl.pallas_call(backward_kernel, out_shape=out)(*args)


def grads_kernel(scale, count, pieces, with_parts, core, pre_l, pre_r, *refs):
    lefts, rights, refs = refs[:pieces], refs[pieces : 2 * pieces], refs[2 * pieces :]
    weights, controls, refs = refs[: 2 * count], refs[2 * count : 4 * count], refs[4 * count :]
    mine, other, local, *parts = refs
    terms = []
    for side, pre, blocks in ((0, pre_l, lefts), (1, pre_r, rights)):
        total = None
        for start, stop, piece in offsets(blocks):
            now = dot_inner(pre[:, start:stop], piece[...])
            total = now if total is None else total + now
        for k in range(count):
            control = controls[2 * k + side][0].astype(F32)
            grad = total[PAD * k : PAD * k + ROWS] * scale
            new = weights[2 * k + side][0].astype(F32) - STEP_SIZE * (grad - control)
            local[side, k] = new
            terms.append(new - STEP_SIZE / PROX_PROB * control)
    first = core[0] == 0
    left = jnp.concatenate(terms[:count], axis=0).astype(BF16)
    right = jnp.concatenate(terms[count:], axis=0).astype(BF16)
    mine[...] = jnp.where(first, left, right)
    other[...] = jnp.where(first, right, left)
    if with_parts:
        g = pl.program_id(0)

        def project(begin):
            for blocks, w, part in ((lefts, weights[0], parts[0]), (rights, weights[1], parts[1])):
                for start, stop, piece in offsets(blocks):
                    now = dot_last(piece[...], w[0])
                    part[start:stop] = now if begin else part[start:stop] + now

        pl.when(g == 0)(lambda: project(True))
        pl.when(g > 0)(lambda: project(False))


WIDTH = HALF // 2


def grads_call(core, pre_l, pre_r, lefts, rights, weights, controls, block, scale, with_parts):
    count = len(weights)
    at = block * WIDTH // BLOCK
    own = at if lefts[0].shape[1] == HALF else 0
    args = (*lefts, *rights)
    specs = [whole(pre_l), whole(pre_r)]
    specs += [pl.BlockSpec((v.shape[0], BLOCK), lambda g: (0, own + g)) for v in args]
    specs += [columns(BLOCK, at), columns(BLOCK, HALF // BLOCK + at)] * (2 * count)
    out = [shaped(count * ROWS, WIDTH, BF16)] * 2
    out_specs = [strips(v) for v in out]
    out += [jax.ShapeDtypeStruct((2, count, ROWS, WIDTH), F32)]
    out_specs += [pl.BlockSpec((2, count, ROWS, BLOCK), lambda g: (0, 0, 0, g))]
    if with_parts:
        sums = [shaped(TOKENS, ROWS, F32)] * 2
        out, out_specs = out + sums, out_specs + [whole(v) for v in sums]
    doubled = [v for v in (*weights, *controls) for _ in range(2)]
    return pl.pallas_call(
        functools.partial(grads_kernel, scale, count, len(lefts), with_parts),
        out_shape=out,
        grid=(WIDTH // BLOCK,),
        in_specs=[pl.BlockSpec(memory_space=pltpu.SMEM)] + specs,
        out_specs=out_specs,
    )(core, pre_l, pre_r, *args, *doubled)


def island_mean(mine, other):
    from_mate = shift(other, core=1)
    pair = (mine.astype(F32) + from_mate.astype(F32)).astype(BF16)
    pair = lax.optimization_barrier(pair)
    across = shift(pair, z_hi=1)
    mean = ((pair.astype(F32) + across.astype(F32)) / 4).astype(BF16)
    return mean, shift(mean, core=1)


def finish_kernel(count, core, mean, mate, local, *refs):
    controls, outs = refs[:count], refs[-2 * count :]
    straight = (core[0] == 0) == (pl.program_id(0) == 0)
    values = jnp.where(straight, mean[...], mate[...]).astype(F32)
    for k in range(count):
        value = values[ROWS * k : ROWS * k + ROWS].astype(BF16)
        outs[2 * k][...] = value
        step = PROX_PROB / STEP_SIZE * (value.astype(F32) - local[0, k])
        outs[2 * k + 1][0] = (controls[k][0].astype(F32) + step).astype(BF16)


def finish_call(core, block, mean, mate, local, controls, before):
    count = len(controls)
    out = [shaped(ROWS, D, BF16), jax.ShapeDtypeStruct((1, ROWS, D), BF16)] * count
    spot = pl.BlockSpec((ROWS, WIDTH), lambda g: (0, 2 * g + block))
    spot3 = pl.BlockSpec((1, ROWS, WIDTH), lambda g: (0, 0, 2 * g + block))
    specs = [pl.BlockSpec(memory_space=pltpu.SMEM), whole(mean), whole(mate)]
    specs += [pl.BlockSpec((1, count, ROWS, WIDTH), lambda g: (g, 0, 0, 0))]
    specs += [spot3] * count + [pl.BlockSpec(memory_space=pl.ANY)] * len(before)
    return pl.pallas_call(
        functools.partial(finish_kernel, count),
        out_shape=out,
        grid=(2,),
        in_specs=specs,
        out_specs=[spot, spot3] * count,
        input_output_aliases={4 + count + i: i for i in range(len(before))},
    )(core, mean, mate, local, *controls, *before)


def per_device(
    activations,
    cotangent,
    gate_weight,
    up_weight,
    down_weight,
    gate_control,
    up_control,
    down_control,
):
    d_scale = D ** (-0.5)
    f_scale = FF ** (-0.5)
    core = jnp.full((1,), lax.axis_index("island") % 2, jnp.int32)
    line = jnp.concatenate(gather_line(normalize(activations[0])), axis=0)
    four_left = jnp.concatenate(ring(line[:, :HALF], "x"), axis=0)
    four_right = jnp.concatenate(ring(line[:, HALF:], "y"), axis=0)
    near_left = relay_near(four_left, "y")
    near_right = relay_near(four_right, "x")
    lefts = relay_far(four_left, near_left, "y")
    rights = relay_far(four_right, near_right, "x")

    rows = cotangent[0]
    ring_left, ring_right = ring(rows[:, :HALF], "x"), ring(rows[:, HALF:], "y")
    cot = []
    for i in range(2):
        at = slice(i * WIDTH, i * WIDTH + WIDTH)
        four = [
            jnp.concatenate([v[:, at] for v in quads], axis=0)
            for quads in (ring_left, ring_right)
        ]
        four = jnp.concatenate(four, axis=1)
        quads = gather_line(four)
        joined = join_call(quads)
        sides = []
        for block, axis in zip(joined, ("y", "x")):
            low = relay_over(block, axis, 1)
            high = relay_over(block, axis, -1)
            far = relay_over(low, axis, 1) if i == 0 else relay_over(high, axis, -1)
            sides.append([block, low, far, high])
        cot.append(sides)

    hidden_l, hidden_r, gate_slope, up_slope = forward_call(lefts, rights, gate_weight, up_weight)
    parts, down = [], []
    for i in range(2):
        mine, other, local, *part = grads_call(
            core, hidden_l, hidden_r, *cot[i], [down_weight], [down_control], i, f_scale, True
        )
        parts.append(part)
        mean, mate = island_mean(mine, other)
        down = finish_call(core, i, mean, mate, local, [down_control], down)
    pre_l, pre_r = backward_call(
        parts[0][0], parts[1][0], parts[0][1], parts[1][1], gate_slope, up_slope
    )
    both = []
    controls = [gate_control, up_control]
    for i in range(2):
        mine, other, local = grads_call(
            core, pre_l, pre_r, lefts, rights, [gate_weight, up_weight], controls, i, d_scale, False
        )
        mean, mate = island_mean(mine, other)
        both = finish_call(core, i, mean, mate, local, controls, both)
    return (both[0], both[2], down[0], both[1], both[3], down[1])


def solution(mesh):
    placed = (P("island", "tensor", None),) * 8
    return jax.shard_map(
        per_device,
        mesh=mesh,
        in_specs=placed,
        out_specs=(P("tensor", None),) * 3 + (P("island", "tensor", None),) * 3,
        check_vma=False,
    )
```
